128 devices in a mesh: row: 8 (over z, core), col: 4 (over y), layer: 4 (over x).
Axes of the slice: x: 4, y: 4, z: 4, core: 2. Of those that a mesh axis runs over, the one named last changes fastest.
Arguments:
- blocks: bfloat16 [512, 24, 128, 128], P(('row', 'col'), 'layer'), may hold values from -2 to 2
- pattern: int32 [512, 24], replicated, may hold values from 0 to 511, as said below
- out_pattern: int32 [512, 24], replicated, may hold values from 0 to 511, as said below
Outputs:
- product: bfloat16 [512, 24, 128, 128], P(('row', 'col'), 'layer')
The draws below stay inside these ranges and needn't reach their ends.
Inputs may be any that keep to these rules, and one draw needn't show every extreme that they name: `pattern`: block row i stores the block columns (i + d) mod 512 for 24 distinct offsets d from -12 to 12, always including 0, -12 and 12, in no particular order. `out_pattern`: the same law as pattern, drawn independently.
All inputs are finite; a program needn't handle non-finite values.
Results may differ from the reference program's by a relative error of at most 0.001.
Values may be sent and summed in bfloat16 or wider, within the bound.
No kernel may reach another device: no remote copies, remote signals or barrier semaphores. Data moves between devices by JAX's collectives and lax.ppermute only.
A program may use at most 192 MiB of HBM per device.

```python
import jax
import jax.numpy as jnp
from jax import lax

BLOCK = 128
SLOTS = 24
REACH = 12
BLOCK_ROWS = 512


def band_pattern(key):
    inner = jnp.concatenate([jnp.arange(-REACH + 1, 0), jnp.arange(1, REACH)]).astype(jnp.int32)
    width = 2 * REACH - 2
    scores = jax.random.randint(jax.random.fold_in(key, 11), (BLOCK_ROWS, width), 0, 2 ** 20)
    scores = scores * width + jnp.arange(width, dtype=jnp.int32)[None, :]
    picks = jnp.argsort(scores, axis=1)[:, :SLOTS - 3]
    chosen = jnp.take(inner, picks)
    fixed = jnp.broadcast_to(jnp.array([0, -REACH, REACH], jnp.int32)[None, :], (BLOCK_ROWS, 3))
    offsets = jnp.concatenate([fixed, chosen], axis=1)
    order = jax.random.randint(jax.random.fold_in(key, 12), (BLOCK_ROWS, SLOTS), 0, 2 ** 20)
    order = order * SLOTS + jnp.arange(SLOTS, dtype=jnp.int32)[None, :]
    offsets = jnp.take_along_axis(offsets, jnp.argsort(order, axis=1), axis=1)
    rows = jnp.arange(BLOCK_ROWS, dtype=jnp.int32)[:, None]
    return ((rows + offsets) % BLOCK_ROWS).astype(jnp.int32)


def draw_pattern(key, part):
    return band_pattern(jax.random.fold_in(key, 1))


def draw_out_pattern(key, part):
    return band_pattern(jax.random.fold_in(key, 2))


def steps_of(own_key, dims, shards, smallest, top_value):
    level = 1.0
    for position, shards_of in shards:
        draws = jax.random.uniform(jax.random.fold_in(jax.random.fold_in(own_key, 6), position), (shards_of,), jnp.float32, smallest / len(shards), top_value / len(shards))
        level = level * jnp.repeat(jnp.exp(draws), dims[position] // shards_of).reshape((-1,) + (1,) * (len(dims) - 1 - position))
    return level


def scatter_about(stream_key, extent, scale, limit, split=(), held_as=jnp.bfloat16):
    values = jax.random.normal(stream_key, extent, jnp.float32) * scale
    if len(split) > 0:
        values = steps_of(stream_key, extent, split, -0.22, 0.18) * values
    return jnp.clip(values, min=-limit, max=limit).astype(held_as)


def setup_inputs(seed: int = 0) -> dict:
    arg_keys = jax.random.split(jax.random.key(seed), 4)
    blocks = scatter_about(arg_keys[0], (BLOCK_ROWS, SLOTS, BLOCK, BLOCK), 0.14, 2.0, ((0, 32), (1, 4)))
    pattern = draw_pattern(jax.random.fold_in(arg_keys[3], 71), 0)
    out_pattern = draw_out_pattern(jax.random.fold_in(arg_keys[3], 71), 0)
    return {"blocks": blocks, "pattern": pattern, "out_pattern": out_pattern}


def reference(blocks, pattern, out_pattern):
    def one_row(item):
        left, cols, out_cols = item
        right = jnp.take(blocks, cols, axis=0).astype(jnp.float32)
        right_cols = jnp.take(pattern, cols, axis=0)
        prods = jnp.einsum("tab,tubc->tuac", left.astype(jnp.float32), right, precision=lax.Precision.HIGHEST)
        match = (right_cols[:, :, None] == out_cols[None, None, :]).astype(jnp.int32)
        found = jnp.max(match, axis=-1)
        target = jnp.where(found > 0, jnp.argmax(match, axis=-1).astype(jnp.int32), jnp.int32(SLOTS)).astype(jnp.int32)
        sums = jax.ops.segment_sum(prods.reshape((SLOTS * SLOTS, BLOCK, BLOCK)), target.reshape(-1), num_segments=SLOTS + 1)
        return sums[:SLOTS]

    full = lax.map(one_row, (blocks, pattern, out_pattern))
    return full.astype(jnp.bfloat16)
```

```python
import jax
import jax.numpy as jnp
import numpy as np
from jax import lax
from jax.experimental import pallas as pl
from jax.experimental.pallas import tpu as pltpu
from jax.sharding import PartitionSpec as P


AXES = ("row", "col", "layer")
B = 128
SLOTS = 24
TOTAL = 512
WIN = 28
BF = jnp.bfloat16
F32 = jnp.float32

RIGHT = 0
LEFT = RIGHT + 32 * WIN
KEPT = LEFT + 4 * 32
PLACE = KEPT + 4 * SLOTS
HOME = PLACE + 1
ZERO = 576
NEAR = 96


def dev(z, c, y, x):
    return ((2 * z + c) * 4 + y) * 4 + x


def devices():
    return [(z, c, y, x) for z in range(4) for c in range(2) for y in range(4) for x in range(4)]


def is_home(c, x):
    return c == (1 if x >= 2 else 0)


def is_first(x):
    return x in (0, 3)


def after(z, c, y, x):
    if y < 3:
        return (z, c, y + 1, x)
    if x < 2:
        return (z, c, 0, 3 - x)
    return ((z + 1) % 4, c, 0, 3 - x)


def before(z, c, y, x):
    if y > 0:
        return (z, c, y - 1, x)
    if x >= 2:
        return (z, c, 3, 3 - x)
    return ((z - 1) % 4, c, 3, 3 - x)


PAIRS_SHARE = [
    (dev(z, c, y, x), dev(z, c, y, x ^ 1) if is_home(c, x) else dev(z, 1 - c, y, 3 - x))
    for z, c, y, x in devices()
]
PAIRS_PASS = [(dev(z, c, y, x), dev(z, c, y, x ^ 1)) for z, c, y, x in devices() if not is_home(c, x)]
PAIRS_UP = [(dev(*d), dev(*after(*d))) for d in devices()]
PAIRS_DOWN = [(dev(*d), dev(*before(*d))) for d in devices()]
PAIRS_WIDE = [(dev(*d), dev(*(after(*d) if is_first(d[3]) else before(*d)))) for d in devices()]
PAIRS_NARROW = [(dev(*d), dev(*(before(*d) if is_first(d[3]) else after(*d)))) for d in devices()]
PAIRS_RELAY = [(dev(z, c, y, x), dev(z, c, y, x ^ 1)) for z, c, y, x in devices()]
PAIRS_SWAP = [(dev(z, c, y, x), dev(z, 1 - c, y, x)) for z, c, y, x in devices()]
AT_HOME = {dev(z, c, y, x) for z, c, y, x in devices() if is_home(c, x)}


def from_home(pairs):
    return [p for p in pairs if p[0] in AT_HOME]


def from_guest(pairs):
    return [p for p in pairs if p[0] not in AT_HOME]


def pairs_out(k, places):
    pairs = []
    for z in range(4):
        for y in range(4):
            for t in range(2):
                for n in places:
                    chip = ((0, 1), (3, 2))[t][n // 2]
                    pairs.append((dev(z, n % 2, y, chip), dev(z, t, y, n ^ k)))
    return pairs


def send(value, pairs):
    return lax.ppermute(value, AXES, pairs)


class Loads:
    def __init__(self, dest, sems):
        self.dest, self.sems, self.waits = dest, sems, []

    def add(self, choices, at, size):
        q = len(self.waits)
        for flag, src, first in choices:

            def go(src=src, first=first):
                pltpu.make_async_copy(
                    src.at[pl.ds(first, size)], self.dest.at[pl.ds(at, size)], self.sems.at[q]
                ).start()

            if flag is None:
                go()
            else:
                pl.when(flag)(go)
        src, first = choices[0][1:]
        self.waits.append(
            pltpu.make_async_copy(
                src.at[pl.ds(first, size)], self.dest.at[pl.ds(at, size)], self.sems.at[q]
            )
        )

    def wait(self):
        for w in self.waits:
            w.wait()


def products(tab, left, raw, first, depth, put):
    lhs = left[:, : depth * B]

    def pair(p, carry):
        rows = []
        for j in range(depth):
            at = RIGHT + (first + j) * WIN + 2 * p
            rows.append(jnp.concatenate([raw[tab[at]], raw[tab[at + 1]]], axis=1))
        r = jnp.dot(lhs, jnp.concatenate(rows, axis=0), preferred_element_type=F32)
        put(2 * p, r[:, :B])
        put(2 * p + 1, r[:, B:])
        return carry

    lax.fori_loop(0, WIN // 2, pair, 0)


def first_kernel(tab, *refs):
    own, ra, rb, za, zb = (refs[2 * q : 2 * q + 2] for q in range(5))
    halos = (refs[10:16], refs[16:22])
    acc, near, far, raw, left, sems = refs[22:]
    loads = Loads(raw, sems)
    home = tab[HOME] == 1
    away = tab[HOME] == 0
    for side in range(2):
        loads.add([(None, ra[side], 0)], side * 96, 48)
        loads.add([(None, rb[side], 0)], side * 96 + 48, 48)
        here, there = (home, away) if side == 0 else (away, home)
        at = (2 + side) * 96
        loads.add([(here, own[side], 0), (there, za[side], 0)], at, 24)
        loads.add([(here, own[side], 72), (there, za[side], 24)], at + 24, 24)
        loads.add([(here, own[side], 24), (there, zb[side], 0)], at + 48, 48)
    for h, halo in enumerate(halos):
        home, away = tab[HOME + 1 + h] == 1, tab[HOME + 1 + h] == 0
        for side in range(2):
            at = 384 + h * 96
            loads.add([(None, halo[2 + side], 0)], at + side * 24, 24)
            here, there = (home, away) if side == 0 else (away, home)
            loads.add(
                [(here, halo[side], 0), (there, halo[4 + side], 0)], at + (2 + side) * 24, 24
            )
    raw[ZERO] = jnp.zeros((B, B), BF)
    loads.wait()

    def one_row(i, carry):
        rows = pl.ds(pl.multiple_of(i * B, B), B)
        for j in range(32):
            block = raw[tab[LEFT + i * 32 + j]]
            if j < 24:
                left[rows, j * B : (j + 1) * B] = block
            else:
                to = near if j < 28 else far
                to[rows, (j % 4) * B : (j % 4 + 1) * B] = block
        return carry

    lax.fori_loop(0, 4, one_row, 0)

    def put(c, value):
        acc[c] = value

    products(tab, left, raw, 0, 24, put)


def select(tab, total, outs):
    place = tab[PLACE]
    for k in range(4):
        lam = (place ^ k) * 6
        out = outs[k]

        def one_row(i, carry):
            for s in range(6):
                c = tab[KEPT + i * SLOTS + lam + s]
                out[i * 6 + s] = total[c, pl.ds(pl.multiple_of(i * B, B), B)].astype(BF)
            return carry

        lax.fori_loop(0, 4, one_row, 0)


def second_kernel(tab, *refs):
    own, r, z = refs[0:2], refs[2:4], refs[4:6]
    left, acc = refs[6:8]
    outs, total, raw, sems = refs[8:12], refs[12], refs[13], refs[14]
    loads = Loads(raw, sems)
    home, away = tab[HOME + 3] == 1, tab[HOME + 3] == 0
    for side in range(2):
        loads.add([(None, r[side], 0)], side * 24, 24)
        here, there = (home, away) if side == 0 else (away, home)
        loads.add([(here, own[side], 0), (there, z[side], 0)], (2 + side) * 24, 24)
    raw[NEAR] = jnp.zeros((B, B), BF)
    loads.wait()

    def put(c, value):
        total[c] = acc[c] + value

    products(tab, left, raw, 24, 4, put)
    select(tab, total, outs)


def third_kernel(tab, *refs):
    left, acc = refs[4:6]
    outs, raw, total, sems = refs[6:10], refs[10], refs[11], refs[12]
    loads = Loads(raw, sems)
    for q in range(4):
        loads.add([(None, refs[q], 0)], q * 24, 24)
    raw[NEAR] = jnp.zeros((B, B), BF)
    loads.wait()

    def put(c, value):
        total[c] = acc[c] + value

    products(tab, left, raw, 28, 4, put)
    select(tab, total, outs)


def place_kernel(where, *refs):
    early, late, out, sems = refs[:4], refs[4:8], refs[8], refs[9]
    x = where[0]
    for n in range(4):
        for k in range(4):
            src = (early if n in (1, 2) else late)[k]

            @pl.when((x ^ n) == k)
            def _():
                pltpu.make_async_copy(src, out.at[pl.ds(24 * n, 24)], sems.at[n]).start()

    for n in range(4):
        pltpu.make_async_copy(early[0], out.at[pl.ds(24 * n, 24)], sems.at[n]).wait()


ANY = pl.BlockSpec(memory_space=pl.ANY)
VM = pl.BlockSpec(memory_space=pltpu.VMEM)
ACC = jax.ShapeDtypeStruct((WIN, 4 * B, B), F32)
SIDE = jax.ShapeDtypeStruct((4 * B, 4 * B), BF)
OUT = jax.ShapeDtypeStruct((24, B, B), BF)


def call(body, tab, far, near, outs, scratch, vmem, flops, moved):
    single = not isinstance(outs, list)
    return pl.pallas_call(
        body,
        out_shape=outs,
        grid_spec=pltpu.PrefetchScalarGridSpec(
            num_scalar_prefetch=1,
            grid=(),
            in_specs=[ANY] * len(far) + [VM] * len(near),
            out_specs=VM if single else [VM] * len(outs),
            scratch_shapes=scratch,
        ),
        compiler_params=pltpu.CompilerParams(vmem_limit_bytes=vmem * 2**20),
        cost_estimate=pl.CostEstimate(flops=flops, transcendentals=0, bytes_accessed=moved),
    )(tab, *far, *near)


def sems(n):
    return pltpu.SemaphoreType.DMA((n,))


def tables(pattern, out_pattern):
    row = lax.axis_index("row")
    y = lax.axis_index("col")
    x = lax.axis_index("layer")
    c = row % 2
    first = jnp.logical_or(x == 0, x == 3)
    group = ((row // 2) * 2 + (x >= 2).astype(jnp.int32)) * 4 + y
    place = jnp.where(first, 0, 2) + c
    top = 16 * group
    base = top + 4 * place - 12
    near = np.arange(4)
    fixed = np.concatenate([near, near + 12, np.arange(4, 12), near - 4, near + 16])
    sec = jnp.where(first, near - 8, near + 20)
    third = jnp.where(first, near - 12, near + 24)
    rows = (top + jnp.concatenate([jnp.asarray(fixed, jnp.int32), sec, third])) % TOTAL
    found = jnp.take(pattern, rows, axis=0)

    def is_home_of(chip, core):
        return (core == (chip >= 2).astype(jnp.int32)).astype(jnp.int32)

    def held(chip):
        out = []
        for core in (c, 1 - c):
            home = is_home_of(chip, core) == 1
            out.append((jnp.where(home, chip ^ 1, 3 - chip), jnp.where(home, chip, (3 - chip) ^ 1)))
        return [out[0][0], out[1][0], out[0][1], out[1][1]]

    low = jnp.where(y == 0, 3 - x, x)
    high = jnp.where(y == 3, 3 - x, x)
    wide = jnp.where(first, low, high)
    direct, relay = held(wide), held(wide ^ 1)
    lam = jnp.stack(
        [jnp.stack(v) for v in (held(x), held(low), held(high), held(wide), direct[:2] + relay[:2])]
    )
    kind = jnp.sum(
        jnp.where(lam[:, None, :] == jnp.arange(4)[None, :, None], jnp.arange(4), 0), axis=-1
    )
    packs = np.array([16, 4, 4, 4, 4])
    pack = np.repeat(np.arange(5), packs)
    kinds = jnp.repeat(kind, packs, axis=0, total_repeat_length=32)
    start = np.array([0, 384, 480, 0, 0])[pack] + 6 * np.concatenate([np.arange(n) for n in packs])
    per_kind = np.array([96, 24, 24, 24, 24])[pack]
    pos = start[:, None, None] + per_kind[:, None, None] * kinds[:, :, None] + np.arange(6)
    pos = pos.reshape(32, SLOTS)
    empty = np.where(np.arange(32) < 24, ZERO, NEAR)[:, None]
    rel = (found - base) % TOTAL
    hit = rel[:, :, None] == jnp.arange(WIN)
    right = jnp.sum(jnp.where(hit, pos[:, :, None] - empty[:, :, None], 0), axis=1) + empty
    at = jnp.where(place == 0, 0, jnp.where(place == 3, 4, jnp.where(place == 1, 8, 12)))
    mine = lax.dynamic_slice_in_dim(found, at, 4, 0)
    spot = lax.dynamic_slice_in_dim(pos, at, 4, 0)
    hit = mine[:, :, None] == rows
    left = jnp.sum(jnp.where(hit, spot[:, :, None] - ZERO, 0), axis=1) + ZERO
    unit = (top + 4 * place + jnp.arange(4)) % TOTAL
    kept = (jnp.take(out_pattern, unit, axis=0) - base) % TOTAL
    small = jnp.stack(
        [place, is_home_of(x, c), is_home_of(low, c), is_home_of(high, c), is_home_of(wide, c)]
    )
    return jnp.concatenate(
        [right.reshape(-1), left.reshape(-1), kept.reshape(-1), small]
    ).astype(jnp.int32)


def square(blocks, pattern, out_pattern):
    x = lax.axis_index("layer")
    first = jnp.logical_or(x == 0, x == 3)
    tab = tables(pattern, out_pattern)
    own = blocks.reshape(96, B, B)
    unit = jnp.where(first, 24, 0)

    def swap(a, b=PAIRS_SWAP):
        return send(a, b)

    ra = send(jnp.concatenate([own[:24], own[72:]], axis=0), PAIRS_SHARE)
    own_up = send(own[72:], from_home(PAIRS_UP))
    own_down = send(own[:24], from_home(PAIRS_DOWN))
    rb = send(own[24:72], PAIRS_SHARE)
    own_sec = send(lax.dynamic_slice_in_dim(own, 24 + unit, 24, 0), from_home(PAIRS_WIDE))
    own_s = swap(own, from_home(PAIRS_SWAP))

    za = send(ra, PAIRS_PASS)
    r_up, r_down = send(ra[24:], PAIRS_UP), send(ra[:24], PAIRS_DOWN)
    zb = send(rb, PAIRS_PASS)
    rb_unit = lax.dynamic_slice_in_dim(rb, unit, 24, 0)
    rb_other = lax.dynamic_slice_in_dim(rb, 24 - unit, 24, 0)
    r_sec = send(rb_unit, PAIRS_WIDE)
    r_narrow = send(rb_unit, PAIRS_NARROW)
    r_direct = send(rb_other, PAIRS_WIDE)
    z_up, z_down = send(za[24:], from_guest(PAIRS_UP)), send(za[:24], from_guest(PAIRS_DOWN))
    z_sec = send(lax.dynamic_slice_in_dim(zb, unit, 24, 0), from_guest(PAIRS_WIDE))
    r_relay = send(r_narrow, PAIRS_RELAY)

    group = [
        own, own_s,
        ra, swap(ra), rb, swap(rb),
        za, swap(za, from_guest(PAIRS_SWAP)), zb, swap(zb, from_guest(PAIRS_SWAP)),
    ]
    group += [own_up, swap(own_up), r_up, swap(r_up), z_up, swap(z_up)]
    group += [own_down, swap(own_down), r_down, swap(r_down), z_down, swap(z_down)]
    acc, near, far = call(
        first_kernel, tab, group, [], [ACC, SIDE, SIDE],
        [pltpu.VMEM((577, B, B), BF), pltpu.VMEM((4 * B, 24 * B), BF), sems(18)],
        40, 11 * 10**9, 28 * 10**6,
    )
    more = [own_sec, swap(own_sec), r_sec, swap(r_sec), z_sec, swap(z_sec)]
    *ready, acc = call(
        second_kernel, tab, more, [near, acc], [OUT] * 4 + [ACC],
        [pltpu.VMEM((97, B, B), BF), sems(4)],
        26, 2 * 10**9, 20 * 10**6,
    )
    early = [send(r, pairs_out(k, (1, 2))) for k, r in enumerate(ready)]
    more = [r_direct, swap(r_direct), r_relay, swap(r_relay)]
    ready = call(
        third_kernel, tab, more, [far, acc], [OUT] * 4,
        [pltpu.VMEM((97, B, B), BF), pltpu.VMEM((WIN, 4 * B, B), F32), sems(4)],
        26, 2 * 10**9, 14 * 10**6,
    )
    late = [send(r, pairs_out(k, (0, 3))) for k, r in enumerate(ready)]
    out = call(
        place_kernel, x.reshape(1).astype(jnp.int32), early + late, [],
        jax.ShapeDtypeStruct((96, B, B), BF), [sems(4)], 8, 0, 6 * 10**6,
    )
    return out.reshape(16, 6, B, B)


def solution(mesh):
    in_specs = (P(("row", "col"), "layer", None, None), P(), P())
    out_specs = P(("row", "col"), "layer", None, None)
    return jax.shard_map(square, mesh=mesh, in_specs=in_specs, out_specs=out_specs, check_vma=False)
```

```python
import jax
import jax.numpy as jnp
from jax import lax
from jax.experimental import pallas as pl
from jax.experimental.pallas import tpu as pltpu
from jax.sharding import PartitionSpec as P


AXES = ("row", "col", "layer")
B = 128
SLOTS = 24
TOTAL = 512
WIN = 28
BF = jnp.bfloat16
F32 = jnp.float32

RIGHT = 0
LEFT = RIGHT + WIN * WIN
KEPT = LEFT + 4 * WIN
PLACE = KEPT + 4 * SLOTS
FLAGS = PLACE + 1
ZERO = 384


def dev(z, c, y, x):
    return ((2 * z + c) * 4 + y) * 4 + x


def devices():
    return [(z, c, y, x) for z in range(4) for c in range(2) for y in range(4) for x in range(4)]


def is_home(c, x):
    return c == (1 if x >= 2 else 0)


def is_first(x):
    return x in (0, 3)


def after(z, c, y, x):
    if y < 3:
        return (z, c, y + 1, x)
    if x < 2:
        return (z, c, 0, 3 - x)
    return ((z + 1) % 4, c, 0, 3 - x)


def before(z, c, y, x):
    if y > 0:
        return (z, c, y - 1, x)
    if x >= 2:
        return (z, c, 3, 3 - x)
    return ((z - 1) % 4, c, 3, 3 - x)


PAIRS_SHARE = [
    (dev(z, c, y, x), dev(z, c, y, x ^ 1) if is_home(c, x) else dev(z, 1 - c, y, 3 - x))
    for z, c, y, x in devices()
]
PAIRS_PASS = [(dev(z, c, y, x), dev(z, c, y, x ^ 1)) for z, c, y, x in devices() if not is_home(c, x)]
PAIRS_WIDE = [(dev(*d), dev(*(after(*d) if is_first(d[3]) else before(*d)))) for d in devices()]
PAIRS_NARROW = [(dev(*d), dev(*(before(*d) if is_first(d[3]) else after(*d)))) for d in devices()]
PAIRS_RELAY = [(dev(z, c, y, x), dev(z, c, y, x ^ 1)) for z, c, y, x in devices()]
PAIRS_SWAP = [(dev(z, c, y, x), dev(z, 1 - c, y, x)) for z, c, y, x in devices()]
AT_HOME = {dev(z, c, y, x) for z, c, y, x in devices() if is_home(c, x)}


def from_home(pairs):
    return [p for p in pairs if p[0] in AT_HOME]


def from_guest(pairs):
    return [p for p in pairs if p[0] not in AT_HOME]


def reached(pairs, start):
    ends = {p[1] for p in pairs}
    return [p for p in start if p[0] in ends]


def turns(pair):
    return pair[0] % 4 != pair[1] % 4


def straight(pairs):
    ends = {dev(*d): d for d in devices()}
    out = []
    for a, b in pairs:
        z, c, y, x = ends[a]
        out.append((dev(z, 1 - c, y, 3 - x), b))
    return out


def only(pairs, home, turn):
    return [p for p in pairs if (p[0] in AT_HOME) == home and turns(p) == turn]


def over(pairs):
    return reached(pairs, PAIRS_SWAP)


OWN_WIDE = only(PAIRS_WIDE, True, False) + straight(only(PAIRS_WIDE, False, True))
OWN_WIDE2 = only(PAIRS_WIDE, True, True)
SHARED_WIDE = [p for p in PAIRS_WIDE if p[0] in AT_HOME or not turns(p)]
OWN_NARROW = only(PAIRS_NARROW, True, False)
OWN_NARROW2 = only(PAIRS_NARROW, True, True)
STRAIGHT = straight(only(PAIRS_NARROW, False, True))
SHARED_NARROW = from_home(PAIRS_NARROW)
GUEST_NARROW = only(PAIRS_NARROW, False, False)
PASSED_NARROW = from_guest(PAIRS_NARROW)
RELAY = reached(GUEST_NARROW, PAIRS_RELAY)
RELAY2 = reached(STRAIGHT, PAIRS_RELAY)


def pairs_out(k, places):
    pairs = []
    for z in range(4):
        for y in range(4):
            for t in range(2):
                for n in places:
                    chip = ((0, 1), (3, 2))[t][n // 2]
                    pairs.append((dev(z, n % 2, y, chip), dev(z, t, y, n ^ k)))
    return pairs


def send(value, pairs):
    return lax.ppermute(value, AXES, pairs)


class Loads:
    def __init__(self, dest, sems):
        self.dest, self.sems, self.waits = dest, sems, []

    def add(self, choices, at, size, gate=None):
        q = len(self.waits)

        def copy(src, first):
            return pltpu.make_async_copy(
                src.at[pl.ds(first, size)], self.dest.at[pl.ds(at, size)], self.sems.at[q]
            )

        for flag, src, first in choices:
            on = flag if gate is None else gate if flag is None else gate & flag
            if on is None:
                copy(src, first).start()
            else:
                pl.when(on)(lambda src=src, first=first: copy(src, first).start())
        self.waits.append((gate, copy(*choices[0][1:])))

    def wait(self):
        for gate, w in self.waits:
            if gate is None:
                w.wait()
            else:
                pl.when(gate)(w.wait)


def products(tab, left, raw, first, origins, put, after=None):
    def pair(p, carry):
        on = [jnp.where((2 * p + 13 >= o) & (2 * p <= o + 15), 1, 0) for o in origins]
        count = sum(on)
        lead = jnp.where(on[0] == 1, 0, jnp.where(on[1] == 1, 1, 2))
        if len(origins) == 4:
            lead = jnp.where(on[0] + on[1] + on[2] == 0, 3, lead)

        for groups in range(len(origins) + 1):

            @pl.when(count == groups)
            def _():
                if groups == 0:
                    put(2 * p, jnp.zeros((4 * B, B), F32))
                    put(2 * p + 1, jnp.zeros((4 * B, B), F32))
                    return
                lhs = left[:, pl.ds(pl.multiple_of(lead * 4 * B, 4 * B), groups * 4 * B)]
                rows = []
                for j in range(4 * groups):
                    at = RIGHT + (first + 4 * lead + j) * WIN + 2 * p
                    rows.append(jnp.concatenate([raw[tab[at]], raw[tab[at + 1]]], axis=1))
                r = jnp.dot(lhs, jnp.concatenate(rows, axis=0), preferred_element_type=F32)
                put(2 * p, r[:, :B])
                put(2 * p + 1, r[:, B:])

        if after is not None:
            after(p)
        return carry

    lax.fori_loop(0, WIN // 2, pair, 0)


def flags(tab, q, side):
    f = tab[FLAGS + q] if side == 0 else 1 - tab[FLAGS + q]
    return f == 1, f == 0


def first_kernel(tab, *refs):
    own, r, z = (refs[2 * q : 2 * q + 2] for q in range(3))
    acc, far, total, raw, left, sems, done = refs[6:]
    loads = Loads(raw, sems)
    for side in range(2):
        yes, no = flags(tab, 0, side)
        loads.add([(None, r[side], 0)], side * 96, 96)
        loads.add([(yes, own[side], 0), (no, z[side], 0)], (2 + side) * 96, 96)
    raw[ZERO] = jnp.zeros((B, B), BF)
    loads.wait()

    def one_row(i, carry):
        rows = pl.ds(pl.multiple_of(i * B, B), B)
        for j in range(WIN):
            block = raw[tab[LEFT + i * WIN + j]]
            if j < 16:
                left[rows, j * B : (j + 1) * B] = block
            else:
                far[rows, (j - 16) * B : (j - 15) * B] = block
        return carry

    lax.fori_loop(0, 4, one_row, 0)

    def put(c, value):
        total[c] = value

    def leave(p):
        two = pl.ds(2 * p, 2)
        return pltpu.make_async_copy(total.at[two], acc.at[two], done.at[p])

    base = 12 - 4 * tab[PLACE]
    products(tab, left, raw, 0, [base + 4 * g for g in range(4)], put, lambda p: leave(p).start())
    for p in range(WIN // 2):
        leave(p).wait()


def select(tab, total, outs):
    place = tab[PLACE]
    for k in range(4):
        lam = (place ^ k) * 6
        out = outs[k]

        def one_row(i, carry):
            for s in range(6):
                c = tab[KEPT + i * SLOTS + lam + s]
                out[i * 6 + s] = total[c, pl.ds(pl.multiple_of(i * B, B), B)].astype(BF)
            return carry

        lax.fori_loop(0, 4, one_row, 0)


def second_kernel(tab, *refs):
    own_w, own_w2, r_w, relay, relay2 = (refs[2 * q : 2 * q + 2] for q in range(5))
    own_n, own_n2, r_n, r_x, own_x, z_n = (refs[10 + 2 * q : 12 + 2 * q] for q in range(6))
    left, acc = refs[22:24]
    outs, raw, total, sems = refs[24:28], *refs[28:]
    loads = Loads(raw, sems)
    edge = (tab[PLACE] == 0) | (tab[PLACE] == 3)
    inside = jnp.logical_not(edge)
    one = tab[FLAGS + 5]
    for side in range(2):
        yes, no = flags(tab, 1, side)
        turn = tab[FLAGS + 3] == 1
        on = jnp.logical_not(turn)
        for first, size, gate in ((24 * one, 48, None), (48 - 48 * one, 24, edge)):
            loads.add(
                [(yes | on, r_w[side], first), (no & turn, own_w[side], first)],
                side * 72 + first, size, gate,
            )
            loads.add(
                [
                    (yes & on, own_w[side], first), (yes & turn, own_w2[side], first),
                    (no & on, relay[side], first), (no & turn, relay2[side], first),
                ],
                (2 + side) * 72 + first, size, gate,
            )
        yes, no = flags(tab, 2, side)
        turn = tab[FLAGS + 4] == 1
        on = jnp.logical_not(turn)
        first = 48 - 48 * one
        loads.add(
            [(yes, r_n[side], 0), (no & on, r_x[side], first), (no & turn, own_x[side], first)],
            288 + side * 24, 24, inside,
        )
        loads.add(
            [(yes & on, own_n[side], 0), (yes & turn, own_n2[side], 0), (no, z_n[side], 0)],
            288 + (2 + side) * 24, 24, inside,
        )
    raw[ZERO] = jnp.zeros((B, B), BF)
    loads.wait()

    def put(c, value):
        total[c] = acc[c] + value

    base = 12 - 4 * tab[PLACE]
    origins = [jnp.where(4 * g < base, 4 * g, 4 * g + 16) for g in range(3)]
    products(tab, left, raw, 16, origins, put)
    select(tab, total, outs)


def place_kernel(where, *refs):
    parts, out, sems = refs[:4], refs[4], refs[5]
    x = where[0]
    for n in range(4):
        for k in range(4):

            @pl.when((x ^ n) == k)
            def _():
                pltpu.make_async_copy(parts[k], out.at[pl.ds(24 * n, 24)], sems.at[n]).start()

    for n in range(4):
        pltpu.make_async_copy(parts[0], out.at[pl.ds(24 * n, 24)], sems.at[n]).wait()


ANY = pl.BlockSpec(memory_space=pl.ANY)
VM = pl.BlockSpec(memory_space=pltpu.VMEM)
ACC = jax.ShapeDtypeStruct((WIN, 4 * B, B), F32)
SIDE = jax.ShapeDtypeStruct((4 * B, 12 * B), BF)
OUT = jax.ShapeDtypeStruct((24, B, B), BF)


def call(body, tab, far, near, outs, scratch, vmem, flops, moved, leaves=0):
    single = not isinstance(outs, list)
    return pl.pallas_call(
        body,
        out_shape=outs,
        grid_spec=pltpu.PrefetchScalarGridSpec(
            num_scalar_prefetch=1,
            grid=(),
            in_specs=[ANY] * len(far) + [VM] * len(near),
            out_specs=VM if single else [ANY] * leaves + [VM] * (len(outs) - leaves),
            scratch_shapes=scratch,
        ),
        compiler_params=pltpu.CompilerParams(vmem_limit_bytes=vmem * 2**20),
        cost_estimate=pl.CostEstimate(flops=flops, transcendentals=0, bytes_accessed=moved),
    )(tab, *far, *near)


def sems(n):
    return pltpu.SemaphoreType.DMA((n,))


def tables(pattern, out_pattern):
    row = lax.axis_index("row")
    y = lax.axis_index("col")
    x = lax.axis_index("layer")
    c = row % 2
    first = jnp.logical_or(x == 0, x == 3)
    group = ((row // 2) * 2 + (x >= 2).astype(jnp.int32)) * 4 + y
    place = jnp.where(first, 0, 2) + c
    base = 16 * group + 4 * place - 12
    k = jnp.arange(12)
    r = jnp.concatenate([jnp.arange(16), jnp.where(k < 12 - 4 * place, k - 12, k + 4) + 4 * place])
    found = jnp.take(pattern, (16 * group + r) % TOTAL, axis=0)
    kept = jnp.take(out_pattern, (base + 12 + jnp.arange(4)) % TOTAL, axis=0)
    kept = (kept - base) % TOTAL

    def is_home_of(chip, core):
        return (core == (chip >= 2).astype(jnp.int32)).astype(jnp.int32)

    def held(chip):
        out = []
        for core in (c, 1 - c):
            home = is_home_of(chip, core) == 1
            out.append((jnp.where(home, chip ^ 1, 3 - chip), jnp.where(home, chip, (3 - chip) ^ 1)))
        return [out[0][0], out[1][0], out[0][1], out[1][1]]

    low = jnp.where(y == 0, 3 - x, x)
    high = jnp.where(y == 3, 3 - x, x)
    wide = jnp.where(first, low, high)
    narrow = jnp.where(first, high, low)
    lam = jnp.stack([jnp.stack(v) for v in (held(x), held(wide), held(narrow))])
    kind = jnp.sum(
        jnp.where(lam[:, None, :] == jnp.arange(4)[None, :, None], jnp.arange(4), 0), axis=-1
    )
    pack = jnp.where((r >= 0) & (r < 16), 0, jnp.where((r < 0) == first, 1, 2))
    top = jnp.where(pack == 0, 0, jnp.where(pack == 1, jnp.where(first, -12, 16), jnp.where(first, 16, -4)))
    start = jnp.where(pack == 2, 288, 0) + 6 * (r - top)
    step = jnp.where(pack == 0, 96, jnp.where(pack == 1, 72, 24))
    kinds = jnp.sum(
        jnp.where(pack[:, None, None] == jnp.arange(3)[None, :, None], kind[None], 0), axis=1
    )
    pos = start[:, None, None] + step[:, None, None] * kinds[:, :, None] + jnp.arange(6)
    pos = pos.reshape(WIN, SLOTS) - ZERO
    rel = (found - base) % TOTAL
    hit = rel[:, :, None] == jnp.arange(WIN)
    right = jnp.sum(jnp.where(hit, pos[:, :, None], 0), axis=1) + ZERO
    mine = lax.dynamic_slice_in_dim(rel, 4 * place, 4, 0)
    spot = lax.dynamic_slice_in_dim(pos, 4 * place, 4, 0)
    hit = mine[:, :, None] == (r - 4 * place + 12)
    left = jnp.sum(jnp.where(hit, spot[:, :, None], 0), axis=1) + ZERO
    turned = [(v != x).astype(jnp.int32) for v in (wide, narrow)]
    homes = [is_home_of(v, c) for v in (x, wide, narrow)]
    small = jnp.stack([place, *homes, *turned, first.astype(jnp.int32)])
    return jnp.concatenate(
        [right.reshape(-1), left.reshape(-1), kept.reshape(-1), small]
    ).astype(jnp.int32)


def square(blocks, pattern, out_pattern):
    x = lax.axis_index("layer")
    first = jnp.logical_or(x == 0, x == 3)
    tab = tables(pattern, out_pattern)
    own = blocks.reshape(96, B, B)

    def cut(a, at, size, behind=None):
        if behind is not None:
            at, _ = lax.optimization_barrier((at, behind))
        return lax.dynamic_slice_in_dim(a, at, size, 0)

    at_w, at_x, at_n = (jnp.where(first, p, q) for p, q in ((24, 0), (0, 24), (0, 72)))

    r = send(own, PAIRS_SHARE)
    mine_w = cut(own, at_w, 72)
    mine_n = cut(own, at_n, 24, mine_w)
    own_w = send(mine_w, OWN_WIDE)
    own_n = send(mine_n, OWN_NARROW)
    own_x = send(cut(own, at_x, 72, mine_n), STRAIGHT)
    own_s = send(own, from_home(PAIRS_SWAP))

    z = send(r, PAIRS_PASS)
    shared_x = cut(r, at_x, 72)
    r_x = send(shared_x, GUEST_NARROW)
    shared_w = cut(r, at_w, 72, shared_x)
    r_w = send(shared_w, SHARED_WIDE)
    r_n = send(cut(r, at_n, 24, shared_w), SHARED_NARROW)
    own_w2 = send(mine_w, OWN_WIDE2)
    own_n2 = send(mine_n, OWN_NARROW2)
    r_s = send(r, PAIRS_SWAP)
    own_w_s = send(own_w, over(OWN_WIDE))
    own_n_s = send(own_n, over(OWN_NARROW))
    own_x_s = send(own_x, over(STRAIGHT))

    z_s = send(z, from_guest(PAIRS_SWAP))
    relay = send(r_x, RELAY)
    relay2 = send(own_x, RELAY2)
    z_n = send(cut(z, at_n, 24), PASSED_NARROW)
    r_x_s = send(r_x, over(GUEST_NARROW))

    r_n_s = send(r_n, over(SHARED_NARROW))
    own_n2_s = send(own_n2, over(OWN_NARROW2))
    relay2_s = send(relay2, over(RELAY2))
    z_n_s = send(z_n, over(PASSED_NARROW))
    r_w_s = send(r_w, over(SHARED_WIDE))
    own_w2_s = send(own_w2, over(OWN_WIDE2))
    relay_s = send(relay, over(RELAY))

    acc, far = call(
        first_kernel, tab, [own, own_s, r, r_s, z, z_s], [], [ACC, SIDE],
        [
            pltpu.VMEM((WIN, 4 * B, B), F32), pltpu.VMEM((ZERO + 1, B, B), BF),
            pltpu.VMEM((4 * B, 16 * B), BF), sems(4), sems(WIN // 2),
        ],
        32, 8 * 10**9, 22 * 10**6, 1,
    )
    more = [own_w, own_w_s, own_w2, own_w2_s, r_w, r_w_s, relay, relay_s, relay2, relay2_s]
    more += [own_n, own_n_s, own_n2, own_n2_s, r_n, r_n_s, r_x, r_x_s, own_x, own_x_s, z_n, z_n_s]
    ready = call(
        second_kernel, tab, more, [far, acc], [OUT] * 4,
        [pltpu.VMEM((ZERO + 1, B, B), BF), pltpu.VMEM((WIN, 4 * B, B), F32), sems(12)],
        36, 6 * 10**9, 22 * 10**6,
    )
    parts = [send(v, pairs_out(k, range(4))) for k, v in enumerate(ready)]
    out = call(
        place_kernel, x.reshape(1).astype(jnp.int32), parts, [],
        jax.ShapeDtypeStruct((96, B, B), BF), [sems(4)], 8, 0, 6 * 10**6,
    )
    return out.reshape(16, 6, B, B)


def solution(mesh):
    in_specs = (P(("row", "col"), "layer", None, None), P(), P())
    out_specs = P(("row", "col"), "layer", None, None)
    return jax.shard_map(square, mesh=mesh, in_specs=in_specs, out_specs=out_specs, check_vma=False)
```

```python
import jax
import jax.numpy as jnp
from jax import lax
from jax.experimental import pallas as pl
from jax.experimental.pallas import tpu as pltpu
from jax.sharding import PartitionSpec as P


AXES = ("row", "col", "layer")
B = 128
SLOTS = 24
TOTAL = 512
WIN = 28
BF = jnp.bfloat16
F32 = jnp.float32

RIGHT = 0
LEFT = RIGHT + WIN * WIN
KEPT = LEFT + 4 * WIN
PLACE = KEPT + 4 * SLOTS
FLAGS = PLACE + 1
ZERO = 384


def dev(z, c, y, x):
    return ((2 * z + c) * 4 + y) * 4 + x


def devices():
    return [(z, c, y, x) for z in range(4) for c in range(2) for y in range(4) for x in range(4)]


def is_home(c, x):
    return c == (1 if x >= 2 else 0)


def is_first(x):
    return x in (0, 3)


def after(z, c, y, x):
    if y < 3:
        return (z, c, y + 1, x)
    if x < 2:
        return (z, c, 0, 3 - x)
    return ((z + 1) % 4, c, 0, 3 - x)


def before(z, c, y, x):
    if y > 0:
        return (z, c, y - 1, x)
    if x >= 2:
        return (z, c, 3, 3 - x)
    return ((z - 1) % 4, c, 3, 3 - x)


PAIRS_SHARE = [
    (dev(z, c, y, x), dev(z, c, y, x ^ 1) if is_home(c, x) else dev(z, 1 - c, y, 3 - x))
    for z, c, y, x in devices()
]
PAIRS_PASS = [(dev(z, c, y, x), dev(z, c, y, x ^ 1)) for z, c, y, x in devices() if not is_home(c, x)]
PAIRS_WIDE = [(dev(*d), dev(*(after(*d) if is_first(d[3]) else before(*d)))) for d in devices()]
PAIRS_NARROW = [(dev(*d), dev(*(before(*d) if is_first(d[3]) else after(*d)))) for d in devices()]
PAIRS_RELAY = [(dev(z, c, y, x), dev(z, c, y, x ^ 1)) for z, c, y, x in devices()]
PAIRS_SWAP = [(dev(z, c, y, x), dev(z, 1 - c, y, x)) for z, c, y, x in devices()]
AT_HOME = {dev(z, c, y, x) for z, c, y, x in devices() if is_home(c, x)}


def from_home(pairs):
    return [p for p in pairs if p[0] in AT_HOME]


def from_guest(pairs):
    return [p for p in pairs if p[0] not in AT_HOME]


def reached(pairs, start):
    ends = {p[1] for p in pairs}
    return [p for p in start if p[0] in ends]


def turns(pair):
    return pair[0] % 4 != pair[1] % 4


def straight(pairs):
    ends = {dev(*d): d for d in devices()}
    out = []
    for a, b in pairs:
        z, c, y, x = ends[a]
        out.append((dev(z, 1 - c, y, 3 - x), b))
    return out


def only(pairs, home, turn):
    return [p for p in pairs if (p[0] in AT_HOME) == home and turns(p) == turn]


def over(pairs):
    return reached(pairs, PAIRS_SWAP)


OWN_WIDE = only(PAIRS_WIDE, True, False) + straight(only(PAIRS_WIDE, False, True))
OWN_WIDE2 = only(PAIRS_WIDE, True, True)
SHARED_WIDE = [p for p in PAIRS_WIDE if p[0] in AT_HOME or not turns(p)]
OWN_NARROW = only(PAIRS_NARROW, True, False)
OWN_NARROW2 = only(PAIRS_NARROW, True, True)
STRAIGHT = straight(only(PAIRS_NARROW, False, True))
SHARED_NARROW = from_home(PAIRS_NARROW)
GUEST_NARROW = only(PAIRS_NARROW, False, False)
PASSED_NARROW = from_guest(PAIRS_NARROW)
RELAY = reached(GUEST_NARROW, PAIRS_RELAY)
RELAY2 = reached(STRAIGHT, PAIRS_RELAY)


def pairs_out(k, places):
    pairs = []
    for z in range(4):
        for y in range(4):
            for t in range(2):
                for n in places:
                    chip = ((0, 1), (3, 2))[t][n // 2]
                    pairs.append((dev(z, n % 2, y, chip), dev(z, t, y, n ^ k)))
    return pairs


def send(value, pairs):
    return lax.ppermute(value, AXES, pairs)


class Loads:
    def __init__(self, dest, sems):
        self.dest, self.sems, self.waits = dest, sems, []

    def add(self, choices, at, size, gate=None):
        q = len(self.waits)

        def copy(src, first):
            return pltpu.make_async_copy(
                src.at[pl.ds(first, size)], self.dest.at[pl.ds(at, size)], self.sems.at[q]
            )

        for flag, src, first in choices:
            on = flag if gate is None else gate if flag is None else gate & flag
            if on is None:
                copy(src, first).start()
            else:
                pl.when(on)(lambda src=src, first=first: copy(src, first).start())
        self.waits.append((gate, copy(*choices[0][1:])))

    def wait(self):
        for gate, w in self.waits:
            if gate is None:
                w.wait()
            else:
                pl.when(gate)(w.wait)


def products(tab, left, raw, first, origins, put, after=None):
    def pair(p, carry):
        on = [jnp.where((2 * p + 13 >= o) & (2 * p <= o + 15), 1, 0) for o in origins]
        count = sum(on)
        lead = jnp.where(on[0] == 1, 0, jnp.where(on[1] == 1, 1, 2))
        if len(origins) == 4:
            lead = jnp.where(on[0] + on[1] + on[2] == 0, 3, lead)

        for groups in range(len(origins) + 1):

            @pl.when(count == groups)
            def _():
                if groups == 0:
                    if after is not None:
                        put(2 * p, jnp.zeros((4 * B, B), F32))
                        put(2 * p + 1, jnp.zeros((4 * B, B), F32))
                    return
                lhs = left[:, pl.ds(pl.multiple_of(lead * 4 * B, 4 * B), groups * 4 * B)]
                rows = []
                for j in range(4 * groups):
                    at = RIGHT + (first + 4 * lead + j) * WIN + 2 * p
                    rows.append(jnp.concatenate([raw[tab[at]], raw[tab[at + 1]]], axis=1))
                r = jnp.dot(lhs, jnp.concatenate(rows, axis=0), preferred_element_type=F32)
                put(2 * p, r[:, :B])
                put(2 * p + 1, r[:, B:])

        if after is not None:
            after(p)
        return carry

    lax.fori_loop(0, WIN // 2, pair, 0)


def flags(tab, q, side):
    f = tab[FLAGS + q] if side == 0 else 1 - tab[FLAGS + q]
    return f == 1, f == 0


def first_kernel(tab, *refs):
    own, r, z = (refs[2 * q : 2 * q + 2] for q in range(3))
    acc, far, total, raw, left, sems, done = refs[6:]
    loads = Loads(raw, sems)
    for side in range(2):
        yes, no = flags(tab, 0, side)
        loads.add([(None, r[side], 0)], side * 96, 96)
        loads.add([(yes, own[side], 0), (no, z[side], 0)], (2 + side) * 96, 96)
    raw[ZERO] = jnp.zeros((B, B), BF)
    loads.wait()

    def one_row(i, carry):
        rows = pl.ds(pl.multiple_of(i * B, B), B)
        for j in range(WIN):
            block = raw[tab[LEFT + i * WIN + j]]
            if j < 16:
                left[rows, j * B : (j + 1) * B] = block
            else:
                far[rows, (j - 16) * B : (j - 15) * B] = block
        return carry

    lax.fori_loop(0, 4, one_row, 0)

    def put(c, value):
        total[c] = value

    def leave(p):
        two = pl.ds(2 * p, 2)
        return pltpu.make_async_copy(total.at[two], acc.at[two], done.at[p])

    base = 12 - 4 * tab[PLACE]
    products(tab, left, raw, 0, [base + 4 * g for g in range(4)], put, lambda p: leave(p).start())
    for p in range(WIN // 2):
        leave(p).wait()


def select(tab, total, outs):
    place = tab[PLACE]
    for k in range(4):
        lam = (place ^ k) * 6
        out = outs[k]

        def one_row(i, carry):
            for s in range(6):
                c = tab[KEPT + i * SLOTS + lam + s]
                out[i * 6 + s] = total[c, pl.ds(pl.multiple_of(i * B, B), B)].astype(BF)
            return carry

        lax.fori_loop(0, 4, one_row, 0)


def second_kernel(tab, *refs):
    own_w, own_w2, r_w, relay, relay2 = (refs[2 * q : 2 * q + 2] for q in range(5))
    own_n, own_n2, r_n, r_x, own_x, z_n = (refs[10 + 2 * q : 12 + 2 * q] for q in range(6))
    far, acc = refs[22:24]
    outs, raw, total, left, sems, early = refs[24:28], *refs[28:]
    sums = pltpu.make_async_copy(acc, total, early.at[0])
    side_copy = pltpu.make_async_copy(far, left, early.at[1])
    loads = Loads(raw, sems)
    edge = (tab[PLACE] == 0) | (tab[PLACE] == 3)
    inside = jnp.logical_not(edge)
    one = tab[FLAGS + 5]
    for side in range(2):
        yes, no = flags(tab, 1, side)
        turn = tab[FLAGS + 3] == 1
        on = jnp.logical_not(turn)
        for first, size, gate in ((24 * one, 48, None), (48 - 48 * one, 24, edge)):
            loads.add(
                [(yes | on, r_w[side], first), (no & turn, own_w[side], first)],
                side * 72 + first, size, gate,
            )
            loads.add(
                [
                    (yes & on, own_w[side], first), (yes & turn, own_w2[side], first),
                    (no & on, relay[side], first), (no & turn, relay2[side], first),
                ],
                (2 + side) * 72 + first, size, gate,
            )
        yes, no = flags(tab, 2, side)
        turn = tab[FLAGS + 4] == 1
        on = jnp.logical_not(turn)
        first = 48 - 48 * one
        loads.add(
            [(yes, r_n[side], 0), (no & on, r_x[side], first), (no & turn, own_x[side], first)],
            288 + side * 24, 24, inside,
        )
        loads.add(
            [(yes & on, own_n[side], 0), (yes & turn, own_n2[side], 0), (no, z_n[side], 0)],
            288 + (2 + side) * 24, 24, inside,
        )
    raw[ZERO] = jnp.zeros((B, B), BF)
    side_copy.start()
    sums.start()
    loads.wait()
    side_copy.wait()
    sums.wait()

    def put(c, value):
        total[c] += value

    base = 12 - 4 * tab[PLACE]
    origins = [jnp.where(4 * g < base, 4 * g, 4 * g + 16) for g in range(3)]
    products(tab, left, raw, 16, origins, put)
    select(tab, total, outs)


def place_kernel(where, *refs):
    parts, out, sems = refs[:4], refs[4], refs[5]
    x = where[0]
    for n in range(4):
        for k in range(4):

            @pl.when((x ^ n) == k)
            def _():
                pltpu.make_async_copy(parts[k], out.at[pl.ds(24 * n, 24)], sems.at[n]).start()

    for n in range(4):
        pltpu.make_async_copy(parts[0], out.at[pl.ds(24 * n, 24)], sems.at[n]).wait()


ANY = pl.BlockSpec(memory_space=pl.ANY)
VM = pl.BlockSpec(memory_space=pltpu.VMEM)
ACC = jax.ShapeDtypeStruct((WIN, 4 * B, B), F32)
SIDE = jax.ShapeDtypeStruct((4 * B, 12 * B), BF)
OUT = jax.ShapeDtypeStruct((24, B, B), BF)


def call(body, tab, far, near, outs, scratch, vmem, flops, moved, leaves=0):
    single = not isinstance(outs, list)
    return pl.pallas_call(
        body,
        out_shape=outs,
        grid_spec=pltpu.PrefetchScalarGridSpec(
            num_scalar_prefetch=1,
            grid=(),
            in_specs=[ANY] * len(far) + [VM] * len(near),
            out_specs=VM if single else [ANY] * leaves + [VM] * (len(outs) - leaves),
            scratch_shapes=scratch,
        ),
        compiler_params=pltpu.CompilerParams(vmem_limit_bytes=vmem * 2**20),
        cost_estimate=pl.CostEstimate(flops=flops, transcendentals=0, bytes_accessed=moved),
    )(tab, *far, *near)


def sems(n):
    return pltpu.SemaphoreType.DMA((n,))


def tables(pattern, out_pattern):
    row = lax.axis_index("row")
    y = lax.axis_index("col")
    x = lax.axis_index("layer")
    c = row % 2
    first = jnp.logical_or(x == 0, x == 3)
    group = ((row // 2) * 2 + (x >= 2).astype(jnp.int32)) * 4 + y
    place = jnp.where(first, 0, 2) + c
    base = 16 * group + 4 * place - 12
    k = jnp.arange(12)
    r = jnp.concatenate([jnp.arange(16), jnp.where(k < 12 - 4 * place, k - 12, k + 4) + 4 * place])
    found = jnp.take(pattern, (16 * group + r) % TOTAL, axis=0)
    kept = jnp.take(out_pattern, (base + 12 + jnp.arange(4)) % TOTAL, axis=0)
    kept = (kept - base) % TOTAL

    def is_home_of(chip, core):
        return (core == (chip >= 2).astype(jnp.int32)).astype(jnp.int32)

    def held(chip):
        out = []
        for core in (c, 1 - c):
            home = is_home_of(chip, core) == 1
            out.append((jnp.where(home, chip ^ 1, 3 - chip), jnp.where(home, chip, (3 - chip) ^ 1)))
        return [out[0][0], out[1][0], out[0][1], out[1][1]]

    low = jnp.where(y == 0, 3 - x, x)
    high = jnp.where(y == 3, 3 - x, x)
    wide = jnp.where(first, low, high)
    narrow = jnp.where(first, high, low)
    lam = jnp.stack([jnp.stack(v) for v in (held(x), held(wide), held(narrow))])
    kind = jnp.sum(
        jnp.where(lam[:, None, :] == jnp.arange(4)[None, :, None], jnp.arange(4), 0), axis=-1
    )
    pack = jnp.where((r >= 0) & (r < 16), 0, jnp.where((r < 0) == first, 1, 2))
    top = jnp.where(pack == 0, 0, jnp.where(pack == 1, jnp.where(first, -12, 16), jnp.where(first, 16, -4)))
    start = jnp.where(pack == 2, 288, 0) + 6 * (r - top)
    step = jnp.where(pack == 0, 96, jnp.where(pack == 1, 72, 24))
    kinds = jnp.sum(
        jnp.where(pack[:, None, None] == jnp.arange(3)[None, :, None], kind[None], 0), axis=1
    )
    pos = start[:, None, None] + step[:, None, None] * kinds[:, :, None] + jnp.arange(6)
    pos = pos.reshape(WIN, SLOTS) - ZERO
    rel = (found - base) % TOTAL
    hit = rel[:, :, None] == jnp.arange(WIN)
    right = jnp.sum(jnp.where(hit, pos[:, :, None], 0), axis=1) + ZERO
    mine = lax.dynamic_slice_in_dim(rel, 4 * place, 4, 0)
    spot = lax.dynamic_slice_in_dim(pos, 4 * place, 4, 0)
    hit = mine[:, :, None] == (r - 4 * place + 12)
    left = jnp.sum(jnp.where(hit, spot[:, :, None], 0), axis=1) + ZERO
    turned = [(v != x).astype(jnp.int32) for v in (wide, narrow)]
    homes = [is_home_of(v, c) for v in (x, wide, narrow)]
    small = jnp.stack([place, *homes, *turned, first.astype(jnp.int32)])
    return jnp.concatenate(
        [right.reshape(-1), left.reshape(-1), kept.reshape(-1), small]
    ).astype(jnp.int32)


def square(blocks, pattern, out_pattern):
    x = lax.axis_index("layer")
    first = jnp.logical_or(x == 0, x == 3)
    tab = tables(pattern, out_pattern)
    own = blocks.reshape(96, B, B)

    def cut(a, at, size, behind=None):
        if behind is not None:
            at, _ = lax.optimization_barrier((at, behind))
        return lax.dynamic_slice_in_dim(a, at, size, 0)

    at_w, at_x, at_n = (jnp.where(first, p, q) for p, q in ((24, 0), (0, 24), (0, 72)))

    r = send(own, PAIRS_SHARE)
    mine_w = cut(own, at_w, 72)
    mine_n = cut(own, at_n, 24, mine_w)
    own_w = send(mine_w, OWN_WIDE)
    own_n = send(mine_n, OWN_NARROW)
    own_x = send(cut(own, at_x, 72, mine_n), STRAIGHT)
    own_s = send(own, from_home(PAIRS_SWAP))

    z = send(r, PAIRS_PASS)
    shared_x = cut(r, at_x, 72)
    r_x = send(shared_x, GUEST_NARROW)
    shared_w = cut(r, at_w, 72, shared_x)
    r_w = send(shared_w, SHARED_WIDE)
    r_n = send(cut(r, at_n, 24, shared_w), SHARED_NARROW)
    own_w2 = send(mine_w, OWN_WIDE2)
    own_n2 = send(mine_n, OWN_NARROW2)
    r_s = send(r, PAIRS_SWAP)
    own_w_s = send(own_w, over(OWN_WIDE))
    own_n_s = send(own_n, over(OWN_NARROW))
    own_x_s = send(own_x, over(STRAIGHT))

    z_s = send(z, from_guest(PAIRS_SWAP))
    relay = send(r_x, RELAY)
    relay2 = send(own_x, RELAY2)
    z_n = send(cut(z, at_n, 24), PASSED_NARROW)
    r_x_s = send(r_x, over(GUEST_NARROW))

    r_n_s = send(r_n, over(SHARED_NARROW))
    own_n2_s = send(own_n2, over(OWN_NARROW2))
    relay2_s = send(relay2, over(RELAY2))
    z_n_s = send(z_n, over(PASSED_NARROW))
    r_w_s = send(r_w, over(SHARED_WIDE))
    own_w2_s = send(own_w2, over(OWN_WIDE2))
    relay_s = send(relay, over(RELAY))

    acc, far = call(
        first_kernel, tab, [own, own_s, r, r_s, z, z_s], [], [ACC, SIDE],
        [
            pltpu.VMEM((WIN, 4 * B, B), F32), pltpu.VMEM((ZERO + 1, B, B), BF),
            pltpu.VMEM((4 * B, 16 * B), BF), sems(4), sems(WIN // 2),
        ],
        32, 8 * 10**9, 22 * 10**6, 1,
    )
    more = [own_w, own_w_s, own_w2, own_w2_s, r_w, r_w_s, relay, relay_s, relay2, relay2_s]
    more += [own_n, own_n_s, own_n2, own_n2_s, r_n, r_n_s, r_x, r_x_s, own_x, own_x_s, z_n, z_n_s]
    ready = call(
        second_kernel, tab, more + [far, acc], [], [OUT] * 4,
        [
            pltpu.VMEM((ZERO + 1, B, B), BF), pltpu.VMEM((WIN, 4 * B, B), F32),
            pltpu.VMEM((4 * B, 12 * B), BF), sems(12), sems(2),
        ],
        36, 6 * 10**9, 22 * 10**6,
    )
    parts = [send(v, pairs_out(k, range(4))) for k, v in enumerate(ready)]
    out = call(
        place_kernel, x.reshape(1).astype(jnp.int32), parts, [],
        jax.ShapeDtypeStruct((96, B, B), BF), [sems(4)], 8, 0, 6 * 10**6,
    )
    return out.reshape(16, 6, B, B)


def solution(mesh):
    in_specs = (P(("row", "col"), "layer", None, None), P(), P())
    out_specs = P(("row", "col"), "layer", None, None)
    return jax.shard_map(square, mesh=mesh, in_specs=in_specs, out_specs=out_specs, check_vma=False)
```
